32 devices in a mesh: seg: 16 (over z, x, core), blk: 2 (over y).
Axes of the slice: x: 2, y: 2, z: 4, core: 2. Of those that a mesh axis runs over, the one named last changes fastest.
Arguments:
- queries: bfloat16 [4096, 2048], P(('seg', 'blk')), may hold values from -6 to 6
- keys: bfloat16 [4096, 2048], P(('seg', 'blk')), may hold values from -6 to 6
- values: bfloat16 [4096, 2048], P(('seg', 'blk')), may hold values from -6 to 6
- mid_offset: int32 [16], replicated, may hold values from 0 to 15, as said below
- far_offset: int32 [16], replicated, may hold values from 0 to 127, as said below
Outputs:
- attended: bfloat16 [4096, 2048], P(('seg', 'blk'))
The draws below stay inside these ranges and needn't reach their ends.
Inputs may be any that keep to these rules, and one draw needn't show every extreme that they name: `mid_offset`: one head has offset 0 and another 16 - 1. `far_offset`: one head has offset 0 and another 128 - 1.
All inputs are finite; a program needn't handle non-finite values.
Results may differ from the reference program's by a relative error of at most 0.0065.
Values may be sent and summed in bfloat16 or wider, within the bound.
A program may use at most 64 MiB of HBM per device.

```python
import math
import jax
import jax.numpy as jnp
from jax import lax

HEADS = 16
DH = 128
TOK_DEV = 128
MID_RATE = 16
BLOCK_LEN = 256
MID_LEN = 1024
FAR_RATE = 128
SEQ = 4096


def offsets_pair(key):
    mid_values = jax.random.randint(jax.random.fold_in(key, 101), (HEADS,), 0, MID_RATE)
    mid_order = jax.random.permutation(jax.random.fold_in(key, 102), HEADS)
    mid_values = mid_values.at[mid_order[0]].set(MID_RATE - 1).at[mid_order[1]].set(0)
    far_values = jax.random.randint(jax.random.fold_in(key, 103), (HEADS,), 0, FAR_RATE)
    far_order = jax.random.permutation(jax.random.fold_in(key, 104), HEADS)
    far_values = far_values.at[far_order[0]].set(FAR_RATE - 1).at[far_order[1]].set(0)
    return (mid_values.astype(jnp.int32), far_values.astype(jnp.int32))


def anchored(key, is_key):
    mid_values, far_values = offsets_pair(key)
    positions = jnp.arange(SEQ, dtype=jnp.int32)
    residue = positions % FAR_RATE
    block_count = SEQ // FAR_RATE
    half_blocks = block_count // 2
    far_hit = residue[:, None] == far_values[None, :]
    query_field = jnp.clip(jax.random.normal(jax.random.fold_in(key, 201), (SEQ, HEADS, DH), jnp.float32), -5.0, 5.0)
    if is_key == 1:
        own_field = jnp.clip(jax.random.normal(jax.random.fold_in(key, 202), (SEQ, HEADS, DH), jnp.float32), -5.0, 5.0)
        partner_field = 0.7 * jnp.roll(query_field, half_blocks * FAR_RATE, axis=0)
        field = jnp.where(far_hit[..., None], partner_field, own_field)
    else:
        field = query_field
    return field.reshape(SEQ, HEADS * DH).astype(jnp.bfloat16)


def draw_queries(key, part):
    return anchored(key, 0)


def draw_keys(key, part):
    return anchored(key, 1)


def draw_mid_offset(key, part):
    return offsets_pair(key)[0]


def draw_far_offset(key, part):
    return offsets_pair(key)[1]


def block_levels(rng, shape, pieces, smallest, top_value):
    level, own = 1.0, jax.random.fold_in(rng, 6)
    for axis_at, blocks in pieces:
        steps = jnp.exp(jax.random.uniform(jax.random.fold_in(own, axis_at), (blocks,), jnp.float32, smallest / len(pieces), top_value / len(pieces)))
        level = level * jnp.repeat(steps, shape[axis_at] // blocks).reshape([-1 if axis == axis_at else 1 for axis in range(len(shape))])
    return level


def scatter_about(key, shape, scale, limit, pieces=(), kind=jnp.bfloat16):
    entries = jax.random.normal(key, shape, jnp.float32) * scale
    if len(pieces) > 0:
        entries = block_levels(key, shape, pieces, -0.22, 0.18) * entries
    return jnp.clip(entries, min=-limit, max=limit).astype(kind)


def setup_inputs(seed: int = 0) -> dict:
    key_of = jax.random.split(jax.random.key(seed), 6)
    queries = draw_queries(jax.random.fold_in(key_of[5], 71), 0)
    keys = draw_keys(jax.random.fold_in(key_of[5], 71), 0)
    values = scatter_about(key_of[2], (SEQ, HEADS * DH), 1.0, 6.0, ((0, 32),))
    mid_offset = draw_mid_offset(jax.random.fold_in(key_of[5], 71), 0)
    far_offset = draw_far_offset(jax.random.fold_in(key_of[5], 71), 0)
    return {"queries": queries, "keys": keys, "values": values, "mid_offset": mid_offset, "far_offset": far_offset}


very_low = -1e+30

def attend_block(query_rows, key_rows, value_rows):
    score_scale = 1.0 / math.sqrt(query_rows.shape[-1])
    scores = jnp.einsum('qhd,khd->hqk', query_rows.astype(jnp.float32), key_rows.astype(jnp.float32)) * score_scale
    row_top = lax.optimization_barrier(jnp.max(scores, axis=-1))
    weights = jnp.exp(scores - row_top[..., None])
    totals = lax.optimization_barrier(jnp.sum(weights, axis=-1))
    rounded = lax.optimization_barrier(weights.astype(jnp.bfloat16)).astype(jnp.float32)
    mixed = jnp.einsum('hqk,khd->qhd', rounded, value_rows.astype(jnp.float32))
    level_out = mixed / jnp.transpose(totals)[..., None]
    level_lse = jnp.transpose(row_top + jnp.log(totals))
    return (level_out, level_lse)

def pick_rows(field, offsets, rate):
    groups = field.shape[0] // rate
    shaped = field.reshape(groups, rate, field.shape[1], field.shape[2])
    index_rows = jnp.broadcast_to(offsets.astype(jnp.int32)[None, None, :, None], (groups, 1, field.shape[1], field.shape[2]))
    return jnp.take_along_axis(shaped, index_rows, axis=1)[:, 0]

def combine_levels(dense_out, dense_lse, mid_out, mid_lse, far_out, far_lse, mid_offset, far_offset):
    rows = dense_out.shape[0]
    heads = dense_out.shape[1]
    dims = dense_out.shape[2]
    rate = rows // mid_out.shape[0]
    mid_hit = jnp.arange(rate, dtype=jnp.int32)[:, None] == mid_offset.astype(jnp.int32)[None, :]
    mid_full = jnp.where(mid_hit[None, :, :, None], mid_out[:, None], 0.0).reshape(rows, heads, dims)
    mid_lse_full = jnp.where(mid_hit[None], mid_lse[:, None, :], very_low).reshape(rows, heads)
    far_hit = jnp.arange(rows, dtype=jnp.int32)[:, None] == far_offset.astype(jnp.int32)[None, :]
    far_full = jnp.where(far_hit[..., None], far_out[None], 0.0)
    far_lse_full = jnp.where(far_hit, far_lse[None], very_low)
    level_top = jnp.maximum(dense_lse, jnp.maximum(mid_lse_full, far_lse_full))
    dense_weight = jnp.exp(dense_lse - level_top)
    mid_weight = jnp.exp(mid_lse_full - level_top)
    far_weight = jnp.exp(far_lse_full - level_top)
    mixed = dense_weight[..., None] * dense_out + mid_weight[..., None] * mid_full + far_weight[..., None] * far_full
    mixed = mixed / (dense_weight + mid_weight + far_weight)[..., None]
    return mixed.astype(jnp.bfloat16).reshape(rows, heads * dims)

def reference(queries, keys, values, mid_offset, far_offset):
    query_all = queries.reshape(SEQ, HEADS, DH)
    key_all = keys.reshape(SEQ, HEADS, DH)
    value_all = values.reshape(SEQ, HEADS, DH)
    blocks = SEQ // TOK_DEV

    def dense_one(parts):
        return attend_block(parts[0], parts[1], parts[2])
    dense_shape = (SEQ // BLOCK_LEN, BLOCK_LEN, HEADS, DH)
    dense_out, dense_lse = lax.map(dense_one, (query_all.reshape(dense_shape), key_all.reshape(dense_shape), value_all.reshape(dense_shape)))
    dense_out = dense_out.reshape(blocks, TOK_DEV, HEADS, DH)
    dense_lse = dense_lse.reshape(blocks, TOK_DEV, HEADS)
    mid_shape = (SEQ // MID_LEN, MID_LEN // MID_RATE, HEADS, DH)
    mid_query = pick_rows(query_all, mid_offset, MID_RATE).reshape(mid_shape)
    mid_key = pick_rows(key_all, mid_offset, MID_RATE).reshape(mid_shape)
    mid_value = pick_rows(value_all, mid_offset, MID_RATE).reshape(mid_shape)
    mid_out, mid_lse = lax.map(dense_one, (mid_query, mid_key, mid_value))
    mid_out = mid_out.reshape(blocks, TOK_DEV // MID_RATE, HEADS, DH)
    mid_lse = mid_lse.reshape(blocks, TOK_DEV // MID_RATE, HEADS)
    far_out, far_lse = attend_block(pick_rows(query_all, far_offset, FAR_RATE), pick_rows(key_all, far_offset, FAR_RATE), pick_rows(value_all, far_offset, FAR_RATE))

    def combine_one(parts):
        return combine_levels(parts[0], parts[1], parts[2], parts[3], parts[4], parts[5], mid_offset, far_offset)
    attended = lax.map(combine_one, (dense_out, dense_lse, mid_out, mid_lse, far_out, far_lse))
    return attended.reshape(SEQ, HEADS * DH)
```

```python
import functools
import math

import jax
import jax.numpy as jnp
from jax import lax
from jax.experimental import pallas as pl
from jax.experimental.pallas import tpu as pltpu
from jax.sharding import PartitionSpec as P

HEADS = 16
DH = 128
SPAN = 4
MID_RATE = 16
HALF = HEADS // 2
MIDW = HALF * DH
CHUNK = 2
EARLY = 1

very_low = -1e30
MESH = pl.DeviceIdType.MESH
SCALE = math.log2(math.e) / math.sqrt(DH)


def dot_nt(a, b):
    return lax.dot_general(a, b, (((1,), (1,)), ((), ())), preferred_element_type=jnp.float32)


def dot_nn(a, b):
    return jnp.dot(a, b, preferred_element_type=jnp.float32)


def kernel(
    segs, blks, q_hbm, k_hbm, v_hbm, mid_ref, far_ref, out_hbm,
    qbuf, kbuf, vbuf, obuf, pack, far, fnum, ftop, fden,
    load_sem, store_sem, kv_send, kv_recv, y_send, y_recv, s_send, s_recv, z_send, z_recv,
):
    rows = qbuf.shape[0]
    per_dev = rows // MID_RATE
    groups = segs // SPAN
    n_chunks = HEADS // CHUNK
    cw = CHUNK * DH
    seg = lax.axis_index("seg")
    blk = lax.axis_index("blk")
    group = seg // SPAN
    place = seg % SPAN

    blk_peers = [(seg, (blk + k) % blks) for k in range(1, blks)]
    span_peers = [(group * SPAN + (place + k) % SPAN, blk) for k in range(1, SPAN)]
    far_peers = [(((group + k) % groups) * SPAN + place, blk) for k in range(1, groups)]

    barrier = pltpu.get_barrier_semaphore()
    peers = blk_peers + span_peers + far_peers
    for peer in peers:
        pl.semaphore_signal(barrier, inc=1, device_id=peer, device_id_type=MESH)

    loads = [
        pltpu.make_async_copy(k_hbm, kbuf.at[blk], load_sem.at[0]),
        pltpu.make_async_copy(v_hbm, vbuf.at[blk], load_sem.at[1]),
        pltpu.make_async_copy(q_hbm, qbuf, load_sem.at[2]),
    ]
    for load in loads:
        load.start()
    pl.semaphore_wait(barrier, len(peers))

    def kv_copy(k, c, which):
        cols = pl.ds(pl.multiple_of(c * cw, cw), cw)
        src, dst = ((k_hbm, kbuf), (v_hbm, vbuf))[which]
        return pltpu.make_async_remote_copy(
            src_ref=src.at[:, cols],
            dst_ref=dst.at[blk, :, cols],
            send_sem=kv_send.at[k, c, which],
            recv_sem=kv_recv.at[k, c, which],
            device_id=blk_peers[k],
            device_id_type=MESH,
        )

    def start_chunk(c):
        for k in range(blks - 1):
            for which in range(2):
                kv_copy(k, c, which).start()

    for c in range(EARLY):
        start_chunk(c)

    loads[0].wait()
    loads[1].wait()

    row = lax.broadcasted_iota(jnp.int32, (2 * HEADS, rows), 0)
    col = lax.broadcasted_iota(jnp.int32, (2 * HEADS, rows), 1)
    is_mid = row < HEADS
    mid_at = (row % per_dev) * MID_RATE

    def one_hot(h):
        mid_hit = is_mid & (row // per_dev == h // HALF) & (col == mid_at + mid_ref[h])
        far_hit = (row == HEADS + h) & (col == far_ref[h])
        return jnp.where(mid_hit | far_hit, 1.0, 0.0).astype(jnp.bfloat16)

    far_kv = jnp.zeros((HEADS, 2 * DH), jnp.float32)
    hots = []
    for g in range(HALF):
        lo = slice(g * DH, (g + 1) * DH)
        hi = slice((g + HALF) * DH, (g + HALF + 1) * DH)
        hot = jnp.concatenate([one_hot(g), one_hot(g + HALF)], axis=1)
        hots.append(hot)
        field = jnp.concatenate(
            [
                jnp.concatenate([kbuf[blk, :, lo], vbuf[blk, :, lo]], axis=1),
                jnp.concatenate([kbuf[blk, :, hi], vbuf[blk, :, hi]], axis=1),
            ],
            axis=0,
        )
        picked = dot_nn(hot, field)
        mid_kv = picked[:HEADS].astype(jnp.bfloat16)
        pack[place, blk, 0, :, lo] = mid_kv[:, :DH]
        pack[place, blk, 1, :, lo] = mid_kv[:, DH:]
        far_kv = far_kv + picked[HEADS:]
    far_kv = far_kv.astype(jnp.bfloat16)
    pack[place, blk, 0, :, MIDW:] = far_kv[:, :DH]
    pack[place, blk, 1, :, MIDW:] = far_kv[:, DH:]

    y_copies = [
        pltpu.make_async_remote_copy(
            src_ref=pack.at[place, blk],
            dst_ref=pack.at[place, blk],
            send_sem=y_send.at[k],
            recv_sem=y_recv.at[k],
            device_id=blk_peers[k],
            device_id_type=MESH,
        )
        for k in range(blks - 1)
    ]
    for copy in y_copies:
        copy.start()
    for c in range(EARLY, n_chunks):
        start_chunk(c)

    loads[2].wait()
    far_q = jnp.zeros((HEADS, DH), jnp.float32)
    for g in range(HALF):
        lo = slice(g * DH, (g + 1) * DH)
        hi = slice((g + HALF) * DH, (g + HALF + 1) * DH)
        field = jnp.concatenate([qbuf[:, lo], qbuf[:, hi]], axis=0)
        far_q = far_q + dot_nn(hots[g][HEADS:], field)
    far_q = far_q.astype(jnp.bfloat16)

    for copy in y_copies:
        copy.wait_recv()
    s_copies = [
        pltpu.make_async_remote_copy(
            src_ref=pack.at[place],
            dst_ref=pack.at[place],
            send_sem=s_send.at[k],
            recv_sem=s_recv.at[k],
            device_id=span_peers[k],
            device_id_type=MESH,
        )
        for k in range(SPAN - 1)
    ]
    for copy in s_copies:
        copy.start()
    for copy in s_copies:
        copy.wait_recv()

    far[group] = pack[:, :, :, :, MIDW:]
    z_copies = [
        pltpu.make_async_remote_copy(
            src_ref=far.at[group],
            dst_ref=far.at[group],
            send_sem=z_send.at[k],
            recv_sem=z_recv.at[k],
            device_id=far_peers[k],
            device_id_type=MESH,
        )
        for k in range(groups - 1)
    ]
    for copy in z_copies:
        copy.start()
    for copy in z_copies:
        copy.wait_recv()

    n_far = segs * blks * HEADS
    far_keys = far[:, :, :, 0].reshape(n_far, DH)
    far_values = far[:, :, :, 1].reshape(n_far, DH)
    far_scores = dot_nt(far_q, far_keys)
    far_row = lax.broadcasted_iota(jnp.int32, (HEADS, n_far), 0)
    far_col = lax.broadcasted_iota(jnp.int32, (HEADS, n_far), 1)
    far_scores = jnp.where(far_col % HEADS == far_row, far_scores, very_low)
    far_top = jnp.max(far_scores, axis=1, keepdims=True)
    far_weights = jnp.exp2((far_scores - far_top) * SCALE)
    fden[...] = jnp.broadcast_to(jnp.sum(far_weights, axis=1, keepdims=True), (HEADS, DH))
    ftop[...] = jnp.broadcast_to(far_top, (HEADS, DH))
    fnum[...] = dot_nn(far_weights.astype(jnp.bfloat16), far_values)

    n_mid = SPAN * blks * 2 * per_dev
    mid_lane = lax.broadcasted_iota(jnp.int32, (rows, n_mid), 1) % (2 * per_dev) // per_dev
    mid_row = lax.broadcasted_iota(jnp.int32, (rows, n_mid), 0) % MID_RATE
    far_at = lax.broadcasted_iota(jnp.int32, (rows, DH), 0)

    def attend(h):
        cols = pl.ds(pl.multiple_of(h * DH, DH), DH)
        mid_cols = pl.ds(pl.multiple_of(h % HALF * DH, DH), DH)
        query = qbuf[:, cols]
        dense_scores = dot_nt(query, kbuf[:, :, cols].reshape(blks * rows, DH))
        mid_scores = dot_nt(query, pack[:, :, 0, :, mid_cols].reshape(n_mid, DH))
        mid_ok = (mid_lane == h // HALF) & (mid_row == mid_ref[h])
        mid_scores = jnp.where(mid_ok, mid_scores, very_low)
        scores = jnp.concatenate([dense_scores, mid_scores], axis=1)
        one_top = jnp.max(scores, axis=1, keepdims=True)
        far_hit = far_at == far_ref[h]
        far_low = jnp.where(far_hit, ftop[pl.ds(h, 1), :], very_low)
        top = jnp.maximum(one_top, far_low)
        weights = jnp.exp2((scores - top[:, :1]) * SCALE)
        far_weight = jnp.exp2((far_low - top) * SCALE)
        total = jnp.sum(weights, axis=1, keepdims=True) + far_weight * fden[pl.ds(h, 1), :]
        probs = weights.astype(jnp.bfloat16)
        mixed = dot_nn(probs[:, : blks * rows], vbuf[:, :, cols].reshape(blks * rows, DH))
        mixed = mixed + dot_nn(
            probs[:, blks * rows :], pack[:, :, 1, :, mid_cols].reshape(n_mid, DH)
        )
        mixed = mixed + far_weight * fnum[pl.ds(h, 1), :]
        obuf[:, cols] = (mixed / total).astype(jnp.bfloat16)

    def out_copy(c):
        cols = pl.ds(pl.multiple_of(c * cw, cw), cw)
        return pltpu.make_async_copy(obuf.at[:, cols], out_hbm.at[:, cols], store_sem.at[c])

    def chunk_step(c, carry):
        for k in range(blks - 1):
            for which in range(2):
                kv_copy(k, c, which).wait_recv()
        for j in range(CHUNK):
            attend(c * CHUNK + j)
        out_copy(c).start()
        return carry

    lax.fori_loop(0, n_chunks, chunk_step, 0)

    for copy in y_copies + s_copies + z_copies:
        copy.wait_send()

    def finish(c, carry):
        for k in range(blks - 1):
            for which in range(2):
                kv_copy(k, c, which).wait_send()
        out_copy(c).wait()
        return carry

    lax.fori_loop(0, n_chunks, finish, 0)


def on_device(segs, blks, queries, keys, values, mid_offset, far_offset):
    rows, width = queries.shape
    groups = segs // SPAN
    n_chunks = HEADS // CHUNK
    bf16, f32 = jnp.bfloat16, jnp.float32
    dma = pltpu.SemaphoreType.DMA
    any_spec = pl.BlockSpec(memory_space=pl.ANY)
    smem_spec = pl.BlockSpec(memory_space=pltpu.SMEM)
    return pl.pallas_call(
        functools.partial(kernel, segs, blks),
        out_shape=jax.ShapeDtypeStruct((rows, width), bf16),
        in_specs=[any_spec, any_spec, any_spec, smem_spec, smem_spec],
        out_specs=any_spec,
        scratch_shapes=[
            pltpu.VMEM((rows, width), bf16),
            pltpu.VMEM((blks, rows, width), bf16),
            pltpu.VMEM((blks, rows, width), bf16),
            pltpu.VMEM((rows, width), bf16),
            pltpu.VMEM((SPAN, blks, 2, HEADS, MIDW + DH), bf16),
            pltpu.VMEM((groups, SPAN, blks, 2, HEADS, DH), bf16),
            pltpu.VMEM((HEADS, DH), f32),
            pltpu.VMEM((HEADS, DH), f32),
            pltpu.VMEM((HEADS, DH), f32),
            dma((3,)),
            dma((n_chunks,)),
            dma((blks - 1, n_chunks, 2)),
            dma((blks - 1, n_chunks, 2)),
            dma((blks - 1,)),
            dma((blks - 1,)),
            dma((SPAN - 1,)),
            dma((SPAN - 1,)),
            dma((groups - 1,)),
            dma((groups - 1,)),
        ],
        compiler_params=pltpu.CompilerParams(
            collective_id=0, has_side_effects=True, vmem_limit_bytes=63 * 1024 * 1024
        ),
    )(queries, keys, values, mid_offset, far_offset)


def solution(mesh):
    spec = P(("seg", "blk"), None)
    return jax.shard_map(
        functools.partial(on_device, mesh.shape["seg"], mesh.shape["blk"]),
        mesh=mesh,
        in_specs=(spec, spec, spec, P(), P()),
        out_specs=spec,
        check_vma=False,
    )
```

```python
import functools
import math

import jax
import jax.numpy as jnp
from jax import lax
from jax.experimental import pallas as pl
from jax.experimental.pallas import tpu as pltpu
from jax.sharding import PartitionSpec as P

HEADS = 16
DH = 128
SPAN = 4
MID_RATE = 16
HALF = HEADS // 2
MIDW = HALF * DH
CHUNK = 2
EARLY = 1

very_low = -1e30
MESH = pl.DeviceIdType.MESH
SCALE = math.log2(math.e) / math.sqrt(DH)


def dot_nt(a, b):
    return lax.dot_general(a, b, (((1,), (1,)), ((), ())), preferred_element_type=jnp.float32)


def dot_nn(a, b):
    return jnp.dot(a, b, preferred_element_type=jnp.float32)


def kernel(
    segs, blks, q_hbm, k_hbm, v_hbm, mid_ref, far_ref, out_ref,
    qbuf, kbuf, vbuf, pack, far, fnum, ftop, fden,
    load_sem, kv_send, kv_recv, y_send, y_recv, s_send, s_recv, z_send, z_recv,
):
    rows = qbuf.shape[0]
    per_dev = rows // MID_RATE
    groups = segs // SPAN
    n_chunks = HEADS // CHUNK
    cw = CHUNK * DH
    seg = lax.axis_index("seg")
    blk = lax.axis_index("blk")
    group = seg // SPAN
    place = seg % SPAN

    blk_peers = [(seg, (blk + k) % blks) for k in range(1, blks)]
    span_peers = [(group * SPAN + (place + k) % SPAN, blk) for k in range(1, SPAN)]
    far_peers = [(((group + k) % groups) * SPAN + place, blk) for k in range(1, groups)]

    barrier = pltpu.get_barrier_semaphore()
    peers = blk_peers + span_peers + far_peers
    for peer in peers:
        pl.semaphore_signal(barrier, inc=1, device_id=peer, device_id_type=MESH)

    loads = [
        pltpu.make_async_copy(k_hbm, kbuf.at[blk], load_sem.at[0]),
        pltpu.make_async_copy(v_hbm, vbuf.at[blk], load_sem.at[1]),
        pltpu.make_async_copy(q_hbm, qbuf, load_sem.at[2]),
    ]
    for load in loads:
        load.start()
    pl.semaphore_wait(barrier, len(peers))

    def kv_copy(k, c, which):
        cols = pl.ds(pl.multiple_of(c * cw, cw), cw)
        src, dst = ((k_hbm, kbuf), (v_hbm, vbuf))[which]
        return pltpu.make_async_remote_copy(
            src_ref=src.at[:, cols],
            dst_ref=dst.at[blk, :, cols],
            send_sem=kv_send.at[k, c, which],
            recv_sem=kv_recv.at[k, c, which],
            device_id=blk_peers[k],
            device_id_type=MESH,
        )

    def start_chunk(c):
        for k in range(blks - 1):
            for which in range(2):
                kv_copy(k, c, which).start()

    for c in range(EARLY):
        start_chunk(c)

    loads[0].wait()
    loads[1].wait()

    row = lax.broadcasted_iota(jnp.int32, (2 * HEADS, rows), 0)
    col = lax.broadcasted_iota(jnp.int32, (2 * HEADS, rows), 1)
    is_mid = row < HEADS
    mid_at = (row % per_dev) * MID_RATE

    def one_hot(h):
        mid_hit = is_mid & (row // per_dev == h // HALF) & (col == mid_at + mid_ref[h])
        far_hit = (row == HEADS + h) & (col == far_ref[h])
        return jnp.where(mid_hit | far_hit, 1.0, 0.0).astype(jnp.bfloat16)

    far_kv = jnp.zeros((HEADS, 2 * DH), jnp.float32)
    hots = []
    for g in range(HALF):
        lo = slice(g * DH, (g + 1) * DH)
        hi = slice((g + HALF) * DH, (g + HALF + 1) * DH)
        hot = jnp.concatenate([one_hot(g), one_hot(g + HALF)], axis=1)
        hots.append(hot)
        field = jnp.concatenate(
            [
                jnp.concatenate([kbuf[blk, :, lo], vbuf[blk, :, lo]], axis=1),
                jnp.concatenate([kbuf[blk, :, hi], vbuf[blk, :, hi]], axis=1),
            ],
            axis=0,
        )
        picked = dot_nn(hot, field)
        mid_kv = picked[:HEADS].astype(jnp.bfloat16)
        pack[place, blk, 0, :, lo] = mid_kv[:, :DH]
        pack[place, blk, 1, :, lo] = mid_kv[:, DH:]
        far_kv = far_kv + picked[HEADS:]
    far_kv = far_kv.astype(jnp.bfloat16)
    pack[place, blk, 0, :, MIDW:] = far_kv[:, :DH]
    pack[place, blk, 1, :, MIDW:] = far_kv[:, DH:]

    y_copies = [
        pltpu.make_async_remote_copy(
            src_ref=pack.at[place, blk],
            dst_ref=pack.at[place, blk],
            send_sem=y_send.at[k],
            recv_sem=y_recv.at[k],
            device_id=blk_peers[k],
            device_id_type=MESH,
        )
        for k in range(blks - 1)
    ]
    for copy in y_copies:
        copy.start()
    for c in range(EARLY, n_chunks):
        start_chunk(c)

    loads[2].wait()
    far_q = jnp.zeros((HEADS, DH), jnp.float32)
    for g in range(HALF):
        lo = slice(g * DH, (g + 1) * DH)
        hi = slice((g + HALF) * DH, (g + HALF + 1) * DH)
        field = jnp.concatenate([qbuf[:, lo], qbuf[:, hi]], axis=0)
        far_q = far_q + dot_nn(hots[g][HEADS:], field)
    far_q = far_q.astype(jnp.bfloat16)

    for copy in y_copies:
        copy.wait_recv()
    s_copies = [
        pltpu.make_async_remote_copy(
            src_ref=pack.at[place],
            dst_ref=pack.at[place],
            send_sem=s_send.at[k],
            recv_sem=s_recv.at[k],
            device_id=span_peers[k],
            device_id_type=MESH,
        )
        for k in range(SPAN - 1)
    ]
    for copy in s_copies:
        copy.start()
    for copy in s_copies:
        copy.wait_recv()

    far[group] = pack[:, :, :, :, MIDW:]
    z_copies = [
        pltpu.make_async_remote_copy(
            src_ref=far.at[group],
            dst_ref=far.at[group],
            send_sem=z_send.at[k],
            recv_sem=z_recv.at[k],
            device_id=far_peers[k],
            device_id_type=MESH,
        )
        for k in range(groups - 1)
    ]
    for copy in z_copies:
        copy.start()
    for copy in z_copies:
        copy.wait_recv()

    n_far = segs * blks * HEADS
    far_keys = far[:, :, :, 0].reshape(n_far, DH)
    far_values = far[:, :, :, 1].reshape(n_far, DH)
    far_scores = dot_nt(far_q, far_keys)
    far_row = lax.broadcasted_iota(jnp.int32, (HEADS, n_far), 0)
    far_col = lax.broadcasted_iota(jnp.int32, (HEADS, n_far), 1)
    far_scores = jnp.where(far_col % HEADS == far_row, far_scores, very_low)
    far_top = jnp.max(far_scores, axis=1, keepdims=True)
    far_weights = jnp.exp2((far_scores - far_top) * SCALE)
    fden[...] = jnp.broadcast_to(jnp.sum(far_weights, axis=1, keepdims=True), (HEADS, DH))
    ftop[...] = jnp.broadcast_to(far_top, (HEADS, DH))
    fnum[...] = dot_nn(far_weights.astype(jnp.bfloat16), far_values)

    n_mid = SPAN * blks * 2 * per_dev
    mid_lane = lax.broadcasted_iota(jnp.int32, (rows, n_mid), 1) % (2 * per_dev) // per_dev
    mid_row = lax.broadcasted_iota(jnp.int32, (rows, n_mid), 0) % MID_RATE
    far_at = lax.broadcasted_iota(jnp.int32, (rows, DH), 0)

    def attend(h):
        cols = pl.ds(pl.multiple_of(h * DH, DH), DH)
        mid_cols = pl.ds(pl.multiple_of(h % HALF * DH, DH), DH)
        query = qbuf[:, cols]
        dense_scores = dot_nt(query, kbuf[:, :, cols].reshape(blks * rows, DH))
        mid_scores = dot_nt(query, pack[:, :, 0, :, mid_cols].reshape(n_mid, DH))
        mid_ok = (mid_lane == h // HALF) & (mid_row == mid_ref[h])
        mid_scores = jnp.where(mid_ok, mid_scores, very_low)
        scores = jnp.concatenate([dense_scores, mid_scores], axis=1)
        one_top = jnp.max(scores, axis=1, keepdims=True)
        far_hit = far_at == far_ref[h]
        far_low = jnp.where(far_hit, ftop[pl.ds(h, 1), :], very_low)
        top = jnp.maximum(one_top, far_low)
        weights = jnp.exp2((scores - top[:, :1]) * SCALE)
        far_weight = jnp.exp2((far_low - top) * SCALE)
        total = jnp.sum(weights, axis=1, keepdims=True) + far_weight * fden[pl.ds(h, 1), :]
        probs = weights.astype(jnp.bfloat16)
        mixed = dot_nn(probs[:, : blks * rows], vbuf[:, :, cols].reshape(blks * rows, DH))
        mixed = mixed + dot_nn(
            probs[:, blks * rows :], pack[:, :, 1, :, mid_cols].reshape(n_mid, DH)
        )
        mixed = mixed + far_weight * fnum[pl.ds(h, 1), :]
        out_ref[:, cols] = (mixed / total).astype(jnp.bfloat16)

    def chunk_step(c, carry):
        for k in range(blks - 1):
            for which in range(2):
                kv_copy(k, c, which).wait_recv()
        for j in range(CHUNK):
            attend(c * CHUNK + j)
        return carry

    lax.fori_loop(0, n_chunks, chunk_step, 0)

    for copy in y_copies + s_copies + z_copies:
        copy.wait_send()

    def finish(c, carry):
        for k in range(blks - 1):
            for which in range(2):
                kv_copy(k, c, which).wait_send()
        return carry

    lax.fori_loop(0, n_chunks, finish, 0)


def on_device(segs, blks, queries, keys, values, mid_offset, far_offset):
    rows, width = queries.shape
    groups = segs // SPAN
    n_chunks = HEADS // CHUNK
    bf16, f32 = jnp.bfloat16, jnp.float32
    dma = pltpu.SemaphoreType.DMA
    any_spec = pl.BlockSpec(memory_space=pl.ANY)
    smem_spec = pl.BlockSpec(memory_space=pltpu.SMEM)
    return pl.pallas_call(
        functools.partial(kernel, segs, blks),
        out_shape=pltpu.VMEM((rows, width), bf16),
        in_specs=[any_spec, any_spec, any_spec, smem_spec, smem_spec],
        out_specs=pl.BlockSpec(memory_space=pltpu.VMEM),
        scratch_shapes=[
            pltpu.VMEM((rows, width), bf16),
            pltpu.VMEM((blks, rows, width), bf16),
            pltpu.VMEM((blks, rows, width), bf16),
            pltpu.VMEM((SPAN, blks, 2, HEADS, MIDW + DH), bf16),
            pltpu.VMEM((groups, SPAN, blks, 2, HEADS, DH), bf16),
            pltpu.VMEM((HEADS, DH), f32),
            pltpu.VMEM((HEADS, DH), f32),
            pltpu.VMEM((HEADS, DH), f32),
            dma((3,)),
            dma((blks - 1, n_chunks, 2)),
            dma((blks - 1, n_chunks, 2)),
            dma((blks - 1,)),
            dma((blks - 1,)),
            dma((SPAN - 1,)),
            dma((SPAN - 1,)),
            dma((groups - 1,)),
            dma((groups - 1,)),
        ],
        compiler_params=pltpu.CompilerParams(
            collective_id=0, has_side_effects=True, vmem_limit_bytes=62 * 1024 * 1024
        ),
    )(queries, keys, values, mid_offset, far_offset)


def solution(mesh):
    spec = P(("seg", "blk"), None)
    return jax.shard_map(
        functools.partial(on_device, mesh.shape["seg"], mesh.shape["blk"]),
        mesh=mesh,
        in_specs=(spec, spec, spec, P(), P()),
        out_specs=spec,
        check_vma=False,
    )
```

```python
import functools
import math

import jax
import jax.numpy as jnp
from jax import lax
from jax.experimental import pallas as pl
from jax.experimental.pallas import tpu as pltpu
from jax.sharding import PartitionSpec as P

HEADS = 16
DH = 128
SPAN = 4
MID_RATE = 16
HALF = HEADS // 2
MIDW = HALF * DH
CHUNK = 2
EARLY = 1

very_low = -1e30
MESH = pl.DeviceIdType.MESH
SCALE = math.log2(math.e) / math.sqrt(DH)


def dot_nt(a, b):
    return lax.dot_general(a, b, (((1,), (1,)), ((), ())), preferred_element_type=jnp.float32)


def dot_nn(a, b):
    return jnp.dot(a, b, preferred_element_type=jnp.float32)


def kernel(
    segs, blks, q_hbm, k_hbm, v_hbm, mid_ref, far_ref, out_ref,
    qbuf, kbuf, vbuf, pack, far, fnum, ftop, fden,
    hello_sem, wide_sem, load_sem, kv_send, kv_recv, y_send, y_recv, s_send, s_recv, z_send, z_recv,
):
    rows = qbuf.shape[0]
    per_dev = rows // MID_RATE
    groups = segs // SPAN
    n_chunks = HEADS // CHUNK
    cw = CHUNK * DH
    seg = lax.axis_index("seg")
    blk = lax.axis_index("blk")
    group = seg // SPAN
    place = seg % SPAN

    blk_peers = [(seg, (blk + k) % blks) for k in range(1, blks)]
    span_peers = [(group * SPAN + (place + k) % SPAN, blk) for k in range(1, SPAN)]
    far_peers = [(((group + k) % groups) * SPAN + place, blk) for k in range(1, groups)]

    barrier = pltpu.get_barrier_semaphore()
    wide = span_peers + far_peers
    paired = blks == 2

    def greet(sem, devices):
        for device in devices:
            pl.semaphore_signal(sem, inc=1, device_id=device, device_id_type=MESH)

    if paired:

        @pl.when(blk == 1)
        def _():
            greet(barrier, blk_peers)
    else:
        greet(barrier, blk_peers + wide)

    loads = [
        pltpu.make_async_copy(k_hbm, kbuf.at[blk], load_sem.at[0]),
        pltpu.make_async_copy(v_hbm, vbuf.at[blk], load_sem.at[1]),
        pltpu.make_async_copy(q_hbm, qbuf, load_sem.at[2]),
    ]
    for load in loads:
        load.start()
    if paired:

        @pl.when(blk == 0)
        def _():
            pl.semaphore_wait(barrier, 1)
            greet(hello_sem, blk_peers)

        @pl.when(blk == 1)
        def _():
            pl.semaphore_wait(hello_sem, 1)
            greet(barrier, wide)
    else:
        pl.semaphore_wait(barrier, len(blk_peers) + len(wide))

    def kv_copy(k, c, which):
        cols = pl.ds(pl.multiple_of(c * cw, cw), cw)
        src, dst = ((k_hbm, kbuf), (v_hbm, vbuf))[which]
        return pltpu.make_async_remote_copy(
            src_ref=src.at[:, cols],
            dst_ref=dst.at[blk, :, cols],
            send_sem=kv_send.at[k, c, which],
            recv_sem=kv_recv.at[k, c, which],
            device_id=blk_peers[k],
            device_id_type=MESH,
        )

    def start_chunk(c):
        for k in range(blks - 1):
            for which in range(2):
                kv_copy(k, c, which).start()

    for c in range(EARLY):
        start_chunk(c)

    loads[0].wait()
    loads[1].wait()

    row = lax.broadcasted_iota(jnp.int32, (2 * HEADS, rows), 0)
    col = lax.broadcasted_iota(jnp.int32, (2 * HEADS, rows), 1)
    is_mid = row < HEADS
    mid_at = (row % per_dev) * MID_RATE

    def one_hot(h):
        mid_hit = is_mid & (row // per_dev == h // HALF) & (col == mid_at + mid_ref[h])
        far_hit = (row == HEADS + h) & (col == far_ref[h])
        return jnp.where(mid_hit | far_hit, 1.0, 0.0).astype(jnp.bfloat16)

    far_kv = jnp.zeros((HEADS, 2 * DH), jnp.float32)
    hots = []
    for g in range(HALF):
        lo = slice(g * DH, (g + 1) * DH)
        hi = slice((g + HALF) * DH, (g + HALF + 1) * DH)
        hot = jnp.concatenate([one_hot(g), one_hot(g + HALF)], axis=1)
        hots.append(hot)
        field = jnp.concatenate(
            [
                jnp.concatenate([kbuf[blk, :, lo], vbuf[blk, :, lo]], axis=1),
                jnp.concatenate([kbuf[blk, :, hi], vbuf[blk, :, hi]], axis=1),
            ],
            axis=0,
        )
        picked = dot_nn(hot, field)
        mid_kv = picked[:HEADS].astype(jnp.bfloat16)
        pack[place, blk, 0, :, lo] = mid_kv[:, :DH]
        pack[place, blk, 1, :, lo] = mid_kv[:, DH:]
        far_kv = far_kv + picked[HEADS:]
    far_kv = far_kv.astype(jnp.bfloat16)
    pack[place, blk, 0, :, MIDW:] = far_kv[:, :DH]
    pack[place, blk, 1, :, MIDW:] = far_kv[:, DH:]

    y_copies = [
        pltpu.make_async_remote_copy(
            src_ref=pack.at[place, blk],
            dst_ref=pack.at[place, blk],
            send_sem=y_send.at[k],
            recv_sem=y_recv.at[k],
            device_id=blk_peers[k],
            device_id_type=MESH,
        )
        for k in range(blks - 1)
    ]
    for copy in y_copies:
        copy.start()
    for c in range(EARLY, n_chunks):
        start_chunk(c)

    if paired:

        @pl.when(blk == 1)
        def _():
            pl.semaphore_wait(barrier, len(wide))
            greet(wide_sem, blk_peers)

        @pl.when(blk == 0)
        def _():
            pl.semaphore_wait(wide_sem, 1)

    loads[2].wait()
    far_q = jnp.zeros((HEADS, DH), jnp.float32)
    for g in range(HALF):
        lo = slice(g * DH, (g + 1) * DH)
        hi = slice((g + HALF) * DH, (g + HALF + 1) * DH)
        field = jnp.concatenate([qbuf[:, lo], qbuf[:, hi]], axis=0)
        far_q = far_q + dot_nn(hots[g][HEADS:], field)
    far_q = far_q.astype(jnp.bfloat16)

    for copy in y_copies:
        copy.wait_recv()
    s_copies = [
        pltpu.make_async_remote_copy(
            src_ref=pack.at[place],
            dst_ref=pack.at[place],
            send_sem=s_send.at[k],
            recv_sem=s_recv.at[k],
            device_id=span_peers[k],
            device_id_type=MESH,
        )
        for k in range(SPAN - 1)
    ]
    for copy in s_copies:
        copy.start()
    for copy in s_copies:
        copy.wait_recv()

    far[group] = pack[:, :, :, :, MIDW:]
    z_copies = [
        pltpu.make_async_remote_copy(
            src_ref=far.at[group],
            dst_ref=far.at[group],
            send_sem=z_send.at[k],
            recv_sem=z_recv.at[k],
            device_id=far_peers[k],
            device_id_type=MESH,
        )
        for k in range(groups - 1)
    ]
    for copy in z_copies:
        copy.start()
    for copy in z_copies:
        copy.wait_recv()

    n_far = segs * blks * HEADS
    far_keys = far[:, :, :, 0].reshape(n_far, DH)
    far_values = far[:, :, :, 1].reshape(n_far, DH)
    far_scores = dot_nt(far_q, far_keys)
    far_row = lax.broadcasted_iota(jnp.int32, (HEADS, n_far), 0)
    far_col = lax.broadcasted_iota(jnp.int32, (HEADS, n_far), 1)
    far_scores = jnp.where(far_col % HEADS == far_row, far_scores, very_low)
    far_top = jnp.max(far_scores, axis=1, keepdims=True)
    far_weights = jnp.exp2((far_scores - far_top) * SCALE)
    fden[...] = jnp.broadcast_to(jnp.sum(far_weights, axis=1, keepdims=True), (HEADS, DH))
    ftop[...] = jnp.broadcast_to(far_top, (HEADS, DH))
    fnum[...] = dot_nn(far_weights.astype(jnp.bfloat16), far_values)

    n_mid = SPAN * blks * 2 * per_dev
    mid_lane = lax.broadcasted_iota(jnp.int32, (rows, n_mid), 1) % (2 * per_dev) // per_dev
    mid_row = lax.broadcasted_iota(jnp.int32, (rows, n_mid), 0) % MID_RATE
    far_at = lax.broadcasted_iota(jnp.int32, (rows, DH), 0)

    def attend(h):
        cols = pl.ds(pl.multiple_of(h * DH, DH), DH)
        mid_cols = pl.ds(pl.multiple_of(h % HALF * DH, DH), DH)
        query = qbuf[:, cols]
        dense_scores = dot_nt(query, kbuf[:, :, cols].reshape(blks * rows, DH))
        mid_scores = dot_nt(query, pack[:, :, 0, :, mid_cols].reshape(n_mid, DH))
        mid_ok = (mid_lane == h // HALF) & (mid_row == mid_ref[h])
        mid_scores = jnp.where(mid_ok, mid_scores, very_low)
        scores = jnp.concatenate([dense_scores, mid_scores], axis=1)
        one_top = jnp.max(scores, axis=1, keepdims=True)
        far_hit = far_at == far_ref[h]
        far_low = jnp.where(far_hit, ftop[pl.ds(h, 1), :], very_low)
        top = jnp.maximum(one_top, far_low)
        weights = jnp.exp2((scores - top[:, :1]) * SCALE)
        far_weight = jnp.exp2((far_low - top) * SCALE)
        total = jnp.sum(weights, axis=1, keepdims=True) + far_weight * fden[pl.ds(h, 1), :]
        probs = weights.astype(jnp.bfloat16)
        mixed = dot_nn(probs[:, : blks * rows], vbuf[:, :, cols].reshape(blks * rows, DH))
        mixed = mixed + dot_nn(
            probs[:, blks * rows :], pack[:, :, 1, :, mid_cols].reshape(n_mid, DH)
        )
        mixed = mixed + far_weight * fnum[pl.ds(h, 1), :]
        out_ref[:, cols] = (mixed / total).astype(jnp.bfloat16)

    def chunk_step(c, carry):
        for k in range(blks - 1):
            for which in range(2):
                kv_copy(k, c, which).wait_recv()
        for j in range(CHUNK):
            attend(c * CHUNK + j)
        return carry

    lax.fori_loop(0, n_chunks, chunk_step, 0)

    for copy in y_copies + s_copies + z_copies:
        copy.wait_send()

    def finish(c, carry):
        for k in range(blks - 1):
            for which in range(2):
                kv_copy(k, c, which).wait_send()
        return carry

    lax.fori_loop(0, n_chunks, finish, 0)


def on_device(segs, blks, queries, keys, values, mid_offset, far_offset):
    rows, width = queries.shape
    groups = segs // SPAN
    n_chunks = HEADS // CHUNK
    bf16, f32 = jnp.bfloat16, jnp.float32
    dma = pltpu.SemaphoreType.DMA
    any_spec = pl.BlockSpec(memory_space=pl.ANY)
    smem_spec = pl.BlockSpec(memory_space=pltpu.SMEM)
    return pl.pallas_call(
        functools.partial(kernel, segs, blks),
        out_shape=pltpu.VMEM((rows, width), bf16),
        in_specs=[any_spec, any_spec, any_spec, smem_spec, smem_spec],
        out_specs=pl.BlockSpec(memory_space=pltpu.VMEM),
        scratch_shapes=[
            pltpu.VMEM((rows, width), bf16),
            pltpu.VMEM((blks, rows, width), bf16),
            pltpu.VMEM((blks, rows, width), bf16),
            pltpu.VMEM((SPAN, blks, 2, HEADS, MIDW + DH), bf16),
            pltpu.VMEM((groups, SPAN, blks, 2, HEADS, DH), bf16),
            pltpu.VMEM((HEADS, DH), f32),
            pltpu.VMEM((HEADS, DH), f32),
            pltpu.VMEM((HEADS, DH), f32),
            pltpu.SemaphoreType.REGULAR,
            pltpu.SemaphoreType.REGULAR,
            dma((3,)),
            dma((blks - 1, n_chunks, 2)),
            dma((blks - 1, n_chunks, 2)),
            dma((blks - 1,)),
            dma((blks - 1,)),
            dma((SPAN - 1,)),
            dma((SPAN - 1,)),
            dma((groups - 1,)),
            dma((groups - 1,)),
        ],
        compiler_params=pltpu.CompilerParams(
            collective_id=0, has_side_effects=True, vmem_limit_bytes=62 * 1024 * 1024
        ),
    )(queries, keys, values, mid_offset, far_offset)


def solution(mesh):
    spec = P(("seg", "blk"), None)
    return jax.shard_map(
        functools.partial(on_device, mesh.shape["seg"], mesh.shape["blk"]),
        mesh=mesh,
        in_specs=(spec, spec, spec, P(), P()),
        out_specs=spec,
        check_vma=False,
    )
```

```python
import functools
import math

import jax
import jax.numpy as jnp
from jax import lax
from jax.experimental import pallas as pl
from jax.experimental.pallas import tpu as pltpu
from jax.sharding import PartitionSpec as P

HEADS = 16
DH = 128
SPAN = 4
MID_RATE = 16
HALF = HEADS // 2
MIDW = HALF * DH
CHUNK = 2
EARLY = 1
LATE = 1

very_low = -1e30
MESH = pl.DeviceIdType.MESH
SCALE = math.log2(math.e) / math.sqrt(DH)


def dot_nt(a, b):
    return lax.dot_general(a, b, (((1,), (1,)), ((), ())), preferred_element_type=jnp.float32)


def dot_nn(a, b):
    return jnp.dot(a, b, preferred_element_type=jnp.float32)


def kernel(
    segs, blks, q_hbm, k_hbm, v_hbm, mid_ref, far_ref, out_ref,
    qbuf, kbuf, vbuf, mid, far, fnum, ftop, fden, rnum, rtop, rden,
    hello_sem, wide_sem, load_sem, kv_send, kv_recv, y_send, y_recv, s_send, s_recv, z_send, z_recv, f_send, f_recv,
):
    rows = qbuf.shape[0]
    per_dev = rows // MID_RATE
    groups = segs // SPAN
    n_chunks = HEADS // CHUNK
    cw = CHUNK * DH
    seg = lax.axis_index("seg")
    blk = lax.axis_index("blk")
    group = seg // SPAN
    place = seg % SPAN

    blk_peers = [(seg, (blk + k) % blks) for k in range(1, blks)]
    span_peers = [(group * SPAN + (place + k) % SPAN, blk) for k in range(1, SPAN)]
    far_peers = [(((group + k) % groups) * SPAN + place, blk) for k in range(1, groups)]

    barrier = pltpu.get_barrier_semaphore()
    wide = span_peers + far_peers
    paired = blks == 2

    def greet(sem, devices):
        for device in devices:
            pl.semaphore_signal(sem, inc=1, device_id=device, device_id_type=MESH)

    if paired:

        @pl.when(blk == 1)
        def _():
            greet(barrier, blk_peers)
    else:
        greet(barrier, blk_peers + wide)

    loads = [
        pltpu.make_async_copy(k_hbm, kbuf.at[blk], load_sem.at[0]),
        pltpu.make_async_copy(v_hbm, vbuf.at[blk], load_sem.at[1]),
        pltpu.make_async_copy(q_hbm, qbuf, load_sem.at[2]),
    ]
    for load in loads:
        load.start()
    if paired:

        @pl.when(blk == 0)
        def _():
            pl.semaphore_wait(barrier, 1)
            greet(hello_sem, blk_peers)

        @pl.when(blk == 1)
        def _():
            pl.semaphore_wait(hello_sem, 1)
            greet(barrier, wide)
    else:
        pl.semaphore_wait(barrier, len(blk_peers) + len(wide))

    def kv_copy(k, c, which):
        cols = pl.ds(pl.multiple_of(c * cw, cw), cw)
        src, dst = ((k_hbm, kbuf), (v_hbm, vbuf))[which]
        return pltpu.make_async_remote_copy(
            src_ref=src.at[:, cols],
            dst_ref=dst.at[blk, :, cols],
            send_sem=kv_send.at[k, c, which],
            recv_sem=kv_recv.at[k, c, which],
            device_id=blk_peers[k],
            device_id_type=MESH,
        )

    def start_chunk(c):
        for k in range(blks - 1):
            for which in range(2):
                kv_copy(k, c, which).start()

    for c in range(EARLY):
        start_chunk(c)

    loads[0].wait()
    loads[1].wait()

    row = lax.broadcasted_iota(jnp.int32, (2 * HEADS, rows), 0)
    col = lax.broadcasted_iota(jnp.int32, (2 * HEADS, rows), 1)
    is_mid = row < HEADS
    mid_at = (row % per_dev) * MID_RATE

    def one_hot(h):
        mid_hit = is_mid & (row // per_dev == h // HALF) & (col == mid_at + mid_ref[h])
        far_hit = (row == HEADS + h) & (col == far_ref[h])
        return jnp.where(mid_hit | far_hit, 1.0, 0.0).astype(jnp.bfloat16)

    far_kv = jnp.zeros((HEADS, 2 * DH), jnp.float32)
    hots = []
    for g in range(HALF):
        lo = slice(g * DH, (g + 1) * DH)
        hi = slice((g + HALF) * DH, (g + HALF + 1) * DH)
        hot = jnp.concatenate([one_hot(g), one_hot(g + HALF)], axis=1)
        hots.append(hot)
        field = jnp.concatenate(
            [
                jnp.concatenate([kbuf[blk, :, lo], vbuf[blk, :, lo]], axis=1),
                jnp.concatenate([kbuf[blk, :, hi], vbuf[blk, :, hi]], axis=1),
            ],
            axis=0,
        )
        picked = dot_nn(hot, field)
        mid_kv = picked[:HEADS].astype(jnp.bfloat16)
        mid[place, blk, 0, :, lo] = mid_kv[:, :DH]
        mid[place, blk, 1, :, lo] = mid_kv[:, DH:]
        far_kv = far_kv + picked[HEADS:]
    far_kv = far_kv.astype(jnp.bfloat16)
    far[place, group, blk, 0] = far_kv[:, :DH]
    far[place, group, blk, 1] = far_kv[:, DH:]

    def remote(ref, send_sem, recv_sem, device):
        return pltpu.make_async_remote_copy(
            src_ref=ref,
            dst_ref=ref,
            send_sem=send_sem,
            recv_sem=recv_sem,
            device_id=device,
            device_id_type=MESH,
        )

    y_copies = []
    for k in range(blks - 1):
        for i, ref in enumerate((far.at[place, group, blk], mid.at[place, blk])):
            y_copies.append(remote(ref, y_send.at[k, i], y_recv.at[k, i], blk_peers[k]))
    for copy in y_copies:
        copy.start()
    for c in range(EARLY, n_chunks):
        start_chunk(c)

    if paired:

        @pl.when(blk == 1)
        def _():
            pl.semaphore_wait(barrier, len(wide))
            greet(wide_sem, blk_peers)

        @pl.when(blk == 0)
        def _():
            pl.semaphore_wait(wide_sem, 1)

    loads[2].wait()
    far_q = jnp.zeros((HEADS, DH), jnp.float32)
    for g in range(HALF):
        lo = slice(g * DH, (g + 1) * DH)
        hi = slice((g + HALF) * DH, (g + HALF + 1) * DH)
        field = jnp.concatenate([qbuf[:, lo], qbuf[:, hi]], axis=0)
        far_q = far_q + dot_nn(hots[g][HEADS:], field)
    far_q = far_q.astype(jnp.bfloat16)

    for copy in y_copies:
        copy.wait_recv()
    z_copies = [
        remote(far.at[place, group], z_send.at[k], z_recv.at[k], far_peers[k])
        for k in range(groups - 1)
    ]
    s_copies = [
        remote(mid.at[place], s_send.at[k], s_recv.at[k], span_peers[k]) for k in range(SPAN - 1)
    ]
    f_copies = [
        remote(far.at[place], f_send.at[k], f_recv.at[k], span_peers[k]) for k in range(SPAN - 1)
    ]
    for copy in z_copies + s_copies:
        copy.start()
    for copy in z_copies:
        copy.wait_recv()
    for copy in f_copies:
        copy.start()
    for copy in s_copies:
        copy.wait_recv()

    n_mid = SPAN * blks * 2 * per_dev
    mid_lane = lax.broadcasted_iota(jnp.int32, (rows, n_mid), 1) % (2 * per_dev) // per_dev
    mid_row = lax.broadcasted_iota(jnp.int32, (rows, n_mid), 0) % MID_RATE
    far_at = lax.broadcasted_iota(jnp.int32, (rows, DH), 0)

    def attend_far():
        n_far = segs * blks * HEADS
        far_keys = far[:, :, :, 0].reshape(n_far, DH)
        far_values = far[:, :, :, 1].reshape(n_far, DH)
        far_scores = dot_nt(far_q, far_keys)
        far_row = lax.broadcasted_iota(jnp.int32, (HEADS, n_far), 0)
        far_col = lax.broadcasted_iota(jnp.int32, (HEADS, n_far), 1)
        far_scores = jnp.where(far_col % HEADS == far_row, far_scores, very_low)
        far_top = jnp.max(far_scores, axis=1, keepdims=True)
        far_weights = jnp.exp2((far_scores - far_top) * SCALE)
        fden[...] = jnp.broadcast_to(jnp.sum(far_weights, axis=1, keepdims=True), (HEADS, DH))
        ftop[...] = jnp.broadcast_to(far_top, (HEADS, DH))
        fnum[...] = dot_nn(far_weights.astype(jnp.bfloat16), far_values)

    def attend(h, with_far):
        cols = pl.ds(pl.multiple_of(h * DH, DH), DH)
        mid_cols = pl.ds(pl.multiple_of(h % HALF * DH, DH), DH)
        query = qbuf[:, cols]
        dense_scores = dot_nt(query, kbuf[:, :, cols].reshape(blks * rows, DH))
        mid_scores = dot_nt(query, mid[:, :, 0, :, mid_cols].reshape(n_mid, DH))
        mid_ok = (mid_lane == h // HALF) & (mid_row == mid_ref[h])
        mid_scores = jnp.where(mid_ok, mid_scores, very_low)
        scores = jnp.concatenate([dense_scores, mid_scores], axis=1)
        top = jnp.max(scores, axis=1, keepdims=True)
        far_hit = far_at == far_ref[h]
        if with_far:
            far_low = jnp.where(far_hit, ftop[pl.ds(h, 1), :], very_low)
            wide_top = jnp.maximum(top, far_low)
            top = wide_top[:, :1]
        weights = jnp.exp2((scores - top) * SCALE)
        total = jnp.sum(weights, axis=1, keepdims=True)
        probs = weights.astype(jnp.bfloat16)
        mixed = dot_nn(probs[:, : blks * rows], vbuf[:, :, cols].reshape(blks * rows, DH))
        mixed = mixed + dot_nn(
            probs[:, blks * rows :], mid[:, :, 1, :, mid_cols].reshape(n_mid, DH)
        )
        if with_far:
            far_weight = jnp.exp2((far_low - wide_top) * SCALE)
            total = total + far_weight * fden[pl.ds(h, 1), :]
            mixed = mixed + far_weight * fnum[pl.ds(h, 1), :]
        else:
            for ref, value in ((rnum, mixed), (rtop, top), (rden, total)):
                kept = jnp.where(far_hit, value, 0.0)
                ref[pl.ds(h, 1), :] = jnp.sum(kept, axis=0, keepdims=True)
        out_ref[:, cols] = (mixed / total).astype(jnp.bfloat16)

    def merge_far():
        top = jnp.maximum(rtop[...], ftop[...])
        near_weight = jnp.exp2((rtop[...] - top) * SCALE)
        far_weight = jnp.exp2((ftop[...] - top) * SCALE)
        total = near_weight * rden[...] + far_weight * fden[...]
        rnum[...] = (near_weight * rnum[...] + far_weight * fnum[...]) / total

        def put(h, carry):
            cols = pl.ds(pl.multiple_of(h * DH, DH), DH)
            plain = out_ref[:, cols].astype(jnp.float32)
            merged = jnp.where(far_at == far_ref[h], rnum[pl.ds(h, 1), :], plain)
            out_ref[:, cols] = merged.astype(jnp.bfloat16)
            return carry

        lax.fori_loop(0, HEADS - LATE * CHUNK, put, 0, unroll=2)

    def await_chunk(c):
        for k in range(blks - 1):
            for which in range(2):
                kv_copy(k, c, which).wait_recv()

    def chunk_step(c, carry):
        await_chunk(c)
        for j in range(CHUNK):
            attend(c * CHUNK + j, False)
        return carry

    for ref in (rnum, rtop, rden):
        ref[...] = jnp.ones_like(ref)
    lax.fori_loop(0, n_chunks - LATE, chunk_step, 0)
    for copy in f_copies:
        copy.wait_recv()
    attend_far()
    merge_far()
    for c in range(n_chunks - LATE, n_chunks):
        await_chunk(c)
        for j in range(CHUNK):
            attend(c * CHUNK + j, True)

    for copy in y_copies + s_copies + z_copies + f_copies:
        copy.wait_send()

    def finish(c, carry):
        for k in range(blks - 1):
            for which in range(2):
                kv_copy(k, c, which).wait_send()
        return carry

    lax.fori_loop(0, n_chunks, finish, 0)


def on_device(segs, blks, queries, keys, values, mid_offset, far_offset):
    rows, width = queries.shape
    groups = segs // SPAN
    n_chunks = HEADS // CHUNK
    bf16, f32 = jnp.bfloat16, jnp.float32
    dma = pltpu.SemaphoreType.DMA
    any_spec = pl.BlockSpec(memory_space=pl.ANY)
    smem_spec = pl.BlockSpec(memory_space=pltpu.SMEM)
    return pl.pallas_call(
        functools.partial(kernel, segs, blks),
        out_shape=pltpu.VMEM((rows, width), bf16),
        in_specs=[any_spec, any_spec, any_spec, smem_spec, smem_spec],
        out_specs=pl.BlockSpec(memory_space=pltpu.VMEM),
        scratch_shapes=[
            pltpu.VMEM((rows, width), bf16),
            pltpu.VMEM((blks, rows, width), bf16),
            pltpu.VMEM((blks, rows, width), bf16),
            pltpu.VMEM((SPAN, blks, 2, HEADS, MIDW), bf16),
            pltpu.VMEM((SPAN, groups, blks, 2, HEADS, DH), bf16),
            pltpu.VMEM((HEADS, DH), f32),
            pltpu.VMEM((HEADS, DH), f32),
            pltpu.VMEM((HEADS, DH), f32),
            pltpu.VMEM((HEADS, DH), f32),
            pltpu.VMEM((HEADS, DH), f32),
            pltpu.VMEM((HEADS, DH), f32),
            pltpu.SemaphoreType.REGULAR,
            pltpu.SemaphoreType.REGULAR,
            dma((3,)),
            dma((blks - 1, n_chunks, 2)),
            dma((blks - 1, n_chunks, 2)),
            dma((blks - 1, 2)),
            dma((blks - 1, 2)),
            dma((SPAN - 1,)),
            dma((SPAN - 1,)),
            dma((groups - 1,)),
            dma((groups - 1,)),
            dma((SPAN - 1,)),
            dma((SPAN - 1,)),
        ],
        compiler_params=pltpu.CompilerParams(
            collective_id=0, has_side_effects=True, vmem_limit_bytes=62 * 1024 * 1024
        ),
    )(queries, keys, values, mid_offset, far_offset)


def solution(mesh):
    spec = P(("seg", "blk"), None)
    return jax.shard_map(
        functools.partial(on_device, mesh.shape["seg"], mesh.shape["blk"]),
        mesh=mesh,
        in_specs=(spec, spec, spec, P(), P()),
        out_specs=spec,
        check_vma=False,
    )
```

```python
import functools
import math

import jax
import jax.numpy as jnp
from jax import lax
from jax.experimental import pallas as pl
from jax.experimental.pallas import tpu as pltpu
from jax.sharding import PartitionSpec as P

HEADS = 16
DH = 128
SPAN = 4
MID_RATE = 16
HALF = HEADS // 2
MIDW = HALF * DH
CHUNK = 2
EARLY = 1
LATE = 1

very_low = -1e30
MESH = pl.DeviceIdType.MESH
SCALE = math.log2(math.e) / math.sqrt(DH)


def dot_nt(a, b):
    return lax.dot_general(a, b, (((1,), (1,)), ((), ())), preferred_element_type=jnp.float32)


def dot_nn(a, b):
    return jnp.dot(a, b, preferred_element_type=jnp.float32)


def kernel(
    segs, blks, q_hbm, k_hbm, v_hbm, mid_hbm, far_hbm, out_ref,
    mid_ref, far_ref,
    qbuf, kbuf, vbuf, mid, far, fnum, ftop, fden, rnum, rtop, rden,
    hello_sem, wide_sem, load_sem, kv_send, kv_recv, y_send, y_recv, s_send, s_recv, z_send, z_recv, f_send, f_recv,
):
    rows = qbuf.shape[0]
    per_dev = rows // MID_RATE
    groups = segs // SPAN
    n_chunks = HEADS // CHUNK
    cw = CHUNK * DH
    seg = lax.axis_index("seg")
    blk = lax.axis_index("blk")
    group = seg // SPAN
    place = seg % SPAN

    blk_peers = [(seg, (blk + k) % blks) for k in range(1, blks)]
    span_peers = [(group * SPAN + (place + k) % SPAN, blk) for k in range(1, SPAN)]
    far_peers = [(((group + k) % groups) * SPAN + place, blk) for k in range(1, groups)]

    barrier = pltpu.get_barrier_semaphore()
    wide = span_peers + far_peers
    paired = blks == 2

    def greet(sem, devices):
        for device in devices:
            pl.semaphore_signal(sem, inc=1, device_id=device, device_id_type=MESH)

    if paired:

        @pl.when(blk == 1)
        def _():
            greet(barrier, blk_peers)
    else:
        greet(barrier, blk_peers + wide)

    loads = [
        pltpu.make_async_copy(k_hbm, kbuf.at[blk], load_sem.at[0]),
        pltpu.make_async_copy(v_hbm, vbuf.at[blk], load_sem.at[1]),
        pltpu.make_async_copy(q_hbm, qbuf, load_sem.at[2]),
        pltpu.make_async_copy(mid_hbm, mid_ref, load_sem.at[3]),
        pltpu.make_async_copy(far_hbm, far_ref, load_sem.at[4]),
    ]
    for load in loads:
        load.start()
    if paired:

        @pl.when(blk == 0)
        def _():
            pl.semaphore_wait(barrier, 1)
            greet(hello_sem, blk_peers)

        @pl.when(blk == 1)
        def _():
            pl.semaphore_wait(hello_sem, 1)
    else:
        pl.semaphore_wait(barrier, len(blk_peers) + len(wide))

    def kv_copy(k, c, which):
        cols = pl.ds(pl.multiple_of(c * cw, cw), cw)
        src, dst = ((k_hbm, kbuf), (v_hbm, vbuf))[which]
        return pltpu.make_async_remote_copy(
            src_ref=src.at[:, cols],
            dst_ref=dst.at[blk, :, cols],
            send_sem=kv_send.at[k, c, which],
            recv_sem=kv_recv.at[k, c, which],
            device_id=blk_peers[k],
            device_id_type=MESH,
        )

    def start_chunk(c):
        for k in range(blks - 1):
            for which in range(2):
                kv_copy(k, c, which).start()

    for c in range(EARLY):
        start_chunk(c)
    if paired:

        @pl.when(blk == 1)
        def _():
            greet(barrier, wide)

    loads[0].wait()
    loads[1].wait()
    loads[3].wait()
    loads[4].wait()

    row = lax.broadcasted_iota(jnp.int32, (2 * HEADS, rows), 0)
    col = lax.broadcasted_iota(jnp.int32, (2 * HEADS, rows), 1)
    is_mid = row < HEADS
    mid_at = (row % per_dev) * MID_RATE

    def one_hot(h):
        mid_hit = is_mid & (row // per_dev == h // HALF) & (col == mid_at + mid_ref[h])
        far_hit = (row == HEADS + h) & (col == far_ref[h])
        return jnp.where(mid_hit | far_hit, 1.0, 0.0).astype(jnp.bfloat16)

    far_kv = jnp.zeros((HEADS, 2 * DH), jnp.float32)
    hots = []
    for g in range(HALF):
        lo = slice(g * DH, (g + 1) * DH)
        hi = slice((g + HALF) * DH, (g + HALF + 1) * DH)
        hot = jnp.concatenate([one_hot(g), one_hot(g + HALF)], axis=1)
        hots.append(hot)
        field = jnp.concatenate(
            [
                jnp.concatenate([kbuf[blk, :, lo], vbuf[blk, :, lo]], axis=1),
                jnp.concatenate([kbuf[blk, :, hi], vbuf[blk, :, hi]], axis=1),
            ],
            axis=0,
        )
        picked = dot_nn(hot, field)
        mid_kv = picked[:HEADS].astype(jnp.bfloat16)
        mid[place, blk, 0, :, lo] = mid_kv[:, :DH]
        mid[place, blk, 1, :, lo] = mid_kv[:, DH:]
        far_kv = far_kv + picked[HEADS:]
    far_kv = far_kv.astype(jnp.bfloat16)
    far[place, group, blk, 0] = far_kv[:, :DH]
    far[place, group, blk, 1] = far_kv[:, DH:]

    def remote(ref, send_sem, recv_sem, device):
        return pltpu.make_async_remote_copy(
            src_ref=ref,
            dst_ref=ref,
            send_sem=send_sem,
            recv_sem=recv_sem,
            device_id=device,
            device_id_type=MESH,
        )

    y_copies = []
    for k in range(blks - 1):
        for i, ref in enumerate((far.at[place, group, blk], mid.at[place, blk])):
            y_copies.append(remote(ref, y_send.at[k, i], y_recv.at[k, i], blk_peers[k]))
    for copy in y_copies:
        copy.start()
    for c in range(EARLY, n_chunks):
        start_chunk(c)

    if paired:

        @pl.when(blk == 1)
        def _():
            pl.semaphore_wait(barrier, len(wide))
            greet(wide_sem, blk_peers)

        @pl.when(blk == 0)
        def _():
            pl.semaphore_wait(wide_sem, 1)

    loads[2].wait()
    far_q = jnp.zeros((HEADS, DH), jnp.float32)
    for g in range(HALF):
        lo = slice(g * DH, (g + 1) * DH)
        hi = slice((g + HALF) * DH, (g + HALF + 1) * DH)
        field = jnp.concatenate([qbuf[:, lo], qbuf[:, hi]], axis=0)
        far_q = far_q + dot_nn(hots[g][HEADS:], field)
    far_q = far_q.astype(jnp.bfloat16)

    for copy in y_copies:
        copy.wait_recv()
    z_copies = [
        remote(far.at[place, group], z_send.at[k], z_recv.at[k], far_peers[k])
        for k in range(groups - 1)
    ]
    s_copies = [
        remote(mid.at[place], s_send.at[k], s_recv.at[k], span_peers[k]) for k in range(SPAN - 1)
    ]
    f_copies = [
        remote(far.at[place], f_send.at[k], f_recv.at[k], span_peers[k]) for k in range(SPAN - 1)
    ]
    for copy in z_copies + s_copies:
        copy.start()
    for copy in z_copies:
        copy.wait_recv()
    for copy in f_copies:
        copy.start()
    for copy in s_copies:
        copy.wait_recv()

    n_mid = SPAN * blks * 2 * per_dev
    mid_lane = lax.broadcasted_iota(jnp.int32, (rows, n_mid), 1) % (2 * per_dev) // per_dev
    mid_row = lax.broadcasted_iota(jnp.int32, (rows, n_mid), 0) % MID_RATE
    far_at = lax.broadcasted_iota(jnp.int32, (rows, DH), 0)

    def attend_far():
        n_far = segs * blks * HEADS
        far_keys = far[:, :, :, 0].reshape(n_far, DH)
        far_values = far[:, :, :, 1].reshape(n_far, DH)
        far_scores = dot_nt(far_q, far_keys)
        far_row = lax.broadcasted_iota(jnp.int32, (HEADS, n_far), 0)
        far_col = lax.broadcasted_iota(jnp.int32, (HEADS, n_far), 1)
        far_scores = jnp.where(far_col % HEADS == far_row, far_scores, very_low)
        far_top = jnp.max(far_scores, axis=1, keepdims=True)
        far_weights = jnp.exp2((far_scores - far_top) * SCALE)
        fden[...] = jnp.broadcast_to(jnp.sum(far_weights, axis=1, keepdims=True), (HEADS, DH))
        ftop[...] = jnp.broadcast_to(far_top, (HEADS, DH))
        fnum[...] = dot_nn(far_weights.astype(jnp.bfloat16), far_values)

    def attend(h, with_far):
        cols = pl.ds(pl.multiple_of(h * DH, DH), DH)
        mid_cols = pl.ds(pl.multiple_of(h % HALF * DH, DH), DH)
        query = qbuf[:, cols]
        dense_scores = dot_nt(query, kbuf[:, :, cols].reshape(blks * rows, DH))
        mid_scores = dot_nt(query, mid[:, :, 0, :, mid_cols].reshape(n_mid, DH))
        mid_ok = (mid_lane == h // HALF) & (mid_row == mid_ref[h])
        mid_scores = jnp.where(mid_ok, mid_scores, very_low)
        scores = jnp.concatenate([dense_scores, mid_scores], axis=1)
        top = jnp.max(scores, axis=1, keepdims=True)
        far_hit = far_at == far_ref[h]
        if with_far:
            far_low = jnp.where(far_hit, ftop[pl.ds(h, 1), :], very_low)
            wide_top = jnp.maximum(top, far_low)
            top = wide_top[:, :1]
        weights = jnp.exp2((scores - top) * SCALE)
        total = jnp.sum(weights, axis=1, keepdims=True)
        probs = weights.astype(jnp.bfloat16)
        mixed = dot_nn(probs[:, : blks * rows], vbuf[:, :, cols].reshape(blks * rows, DH))
        mixed = mixed + dot_nn(
            probs[:, blks * rows :], mid[:, :, 1, :, mid_cols].reshape(n_mid, DH)
        )
        if with_far:
            far_weight = jnp.exp2((far_low - wide_top) * SCALE)
            total = total + far_weight * fden[pl.ds(h, 1), :]
            mixed = mixed + far_weight * fnum[pl.ds(h, 1), :]
        else:
            for ref, value in ((rnum, mixed), (rtop, top), (rden, total)):
                kept = jnp.where(far_hit, value, 0.0)
                ref[pl.ds(h, 1), :] = jnp.sum(kept, axis=0, keepdims=True)
        out_ref[:, cols] = (mixed / total).astype(jnp.bfloat16)

    def merge_far():
        top = jnp.maximum(rtop[...], ftop[...])
        near_weight = jnp.exp2((rtop[...] - top) * SCALE)
        far_weight = jnp.exp2((ftop[...] - top) * SCALE)
        total = near_weight * rden[...] + far_weight * fden[...]
        rnum[...] = (near_weight * rnum[...] + far_weight * fnum[...]) / total

        def put(h, carry):
            cols = pl.ds(pl.multiple_of(h * DH, DH), DH)
            plain = out_ref[:, cols].astype(jnp.float32)
            merged = jnp.where(far_at == far_ref[h], rnum[pl.ds(h, 1), :], plain)
            out_ref[:, cols] = merged.astype(jnp.bfloat16)
            return carry

        lax.fori_loop(0, HEADS - LATE * CHUNK, put, 0, unroll=2)

    def await_chunk(c):
        for k in range(blks - 1):
            for which in range(2):
                kv_copy(k, c, which).wait_recv()

    def chunk_step(c, carry):
        await_chunk(c)
        for j in range(CHUNK):
            attend(c * CHUNK + j, False)
        return carry

    for ref in (rnum, rtop, rden):
        ref[...] = jnp.ones_like(ref)
    lax.fori_loop(0, n_chunks - LATE, chunk_step, 0)
    for copy in f_copies:
        copy.wait_recv()
    attend_far()
    merge_far()
    for c in range(n_chunks - LATE, n_chunks):
        await_chunk(c)
        for j in range(CHUNK):
            attend(c * CHUNK + j, True)

    for copy in y_copies + s_copies + z_copies + f_copies:
        copy.wait_send()

    def finish(c, carry):
        for k in range(blks - 1):
            for which in range(2):
                kv_copy(k, c, which).wait_send()
        return carry

    lax.fori_loop(0, n_chunks, finish, 0)


def on_device(segs, blks, queries, keys, values, mid_offset, far_offset):
    rows, width = queries.shape
    groups = segs // SPAN
    n_chunks = HEADS // CHUNK
    bf16, f32 = jnp.bfloat16, jnp.float32
    dma = pltpu.SemaphoreType.DMA
    any_spec = pl.BlockSpec(memory_space=pl.ANY)
    return pl.pallas_call(
        functools.partial(kernel, segs, blks),
        out_shape=pltpu.VMEM((rows, width), bf16),
        in_specs=[any_spec] * 5,
        out_specs=pl.BlockSpec(memory_space=pltpu.VMEM),
        scratch_shapes=[
            pltpu.SMEM((HEADS,), jnp.int32),
            pltpu.SMEM((HEADS,), jnp.int32),
            pltpu.VMEM((rows, width), bf16),
            pltpu.VMEM((blks, rows, width), bf16),
            pltpu.VMEM((blks, rows, width), bf16),
            pltpu.VMEM((SPAN, blks, 2, HEADS, MIDW), bf16),
            pltpu.VMEM((SPAN, groups, blks, 2, HEADS, DH), bf16),
            pltpu.VMEM((HEADS, DH), f32),
            pltpu.VMEM((HEADS, DH), f32),
            pltpu.VMEM((HEADS, DH), f32),
            pltpu.VMEM((HEADS, DH), f32),
            pltpu.VMEM((HEADS, DH), f32),
            pltpu.VMEM((HEADS, DH), f32),
            pltpu.SemaphoreType.REGULAR,
            pltpu.SemaphoreType.REGULAR,
            dma((5,)),
            dma((blks - 1, n_chunks, 2)),
            dma((blks - 1, n_chunks, 2)),
            dma((blks - 1, 2)),
            dma((blks - 1, 2)),
            dma((SPAN - 1,)),
            dma((SPAN - 1,)),
            dma((groups - 1,)),
            dma((groups - 1,)),
            dma((SPAN - 1,)),
            dma((SPAN - 1,)),
        ],
        compiler_params=pltpu.CompilerParams(
            collective_id=0, has_side_effects=True, vmem_limit_bytes=62 * 1024 * 1024
        ),
    )(queries, keys, values, mid_offset, far_offset)


def solution(mesh):
    spec = P(("seg", "blk"), None)
    return jax.shard_map(
        functools.partial(on_device, mesh.shape["seg"], mesh.shape["blk"]),
        mesh=mesh,
        in_specs=(spec, spec, spec, P(), P()),
        out_specs=spec,
        check_vma=False,
    )
```

```python
import functools
import math

import jax
import jax.numpy as jnp
from jax import lax
from jax.experimental import pallas as pl
from jax.experimental.pallas import tpu as pltpu
from jax.sharding import PartitionSpec as P

HEADS = 16
DH = 128
SPAN = 4
MID_RATE = 16
HALF = HEADS // 2
MIDW = HALF * DH
CHUNK = 4
EARLY = 1
LATE = 1

very_low = -1e30
MESH = pl.DeviceIdType.MESH
SCALE = math.log2(math.e) / math.sqrt(DH)


def dot_nt(a, b):
    return lax.dot_general(a, b, (((1,), (1,)), ((), ())), preferred_element_type=jnp.float32)


def dot_nn(a, b):
    return jnp.dot(a, b, preferred_element_type=jnp.float32)


def kernel(
    segs, blks, q_hbm, k_hbm, v_hbm, mid_hbm, far_hbm, out_ref,
    mid_ref, far_ref,
    qbuf, kbuf, vbuf, mid, far, fnum, ftop, fden, rnum, rtop, rden,
    hello_sem, wide_sem, load_sem, kv_send, kv_recv, y_send, y_recv, s_send, s_recv, z_send, z_recv, f_send, f_recv,
):
    rows = qbuf.shape[0]
    per_dev = rows // MID_RATE
    groups = segs // SPAN
    n_chunks = HEADS // CHUNK
    cw = CHUNK * DH
    seg = lax.axis_index("seg")
    blk = lax.axis_index("blk")
    group = seg // SPAN
    place = seg % SPAN

    blk_peers = [(seg, (blk + k) % blks) for k in range(1, blks)]
    span_peers = [(group * SPAN + (place + k) % SPAN, blk) for k in range(1, SPAN)]
    far_peers = [(((group + k) % groups) * SPAN + place, blk) for k in range(1, groups)]

    barrier = pltpu.get_barrier_semaphore()
    wide = span_peers + far_peers
    paired = blks == 2

    def greet(sem, devices):
        for device in devices:
            pl.semaphore_signal(sem, inc=1, device_id=device, device_id_type=MESH)

    if paired:

        @pl.when(blk == 1)
        def _():
            greet(barrier, blk_peers)
    else:
        greet(barrier, blk_peers + wide)

    loads = [
        pltpu.make_async_copy(k_hbm, kbuf.at[blk], load_sem.at[0]),
        pltpu.make_async_copy(v_hbm, vbuf.at[blk], load_sem.at[1]),
        pltpu.make_async_copy(q_hbm, qbuf, load_sem.at[2]),
        pltpu.make_async_copy(mid_hbm, mid_ref, load_sem.at[3]),
        pltpu.make_async_copy(far_hbm, far_ref, load_sem.at[4]),
    ]
    for load in loads:
        load.start()
    if paired:

        @pl.when(blk == 0)
        def _():
            pl.semaphore_wait(barrier, 1)
            greet(hello_sem, blk_peers)

        @pl.when(blk == 1)
        def _():
            pl.semaphore_wait(hello_sem, 1)
    else:
        pl.semaphore_wait(barrier, len(blk_peers) + len(wide))

    def kv_copy(k, c, which):
        cols = pl.ds(pl.multiple_of(c * cw, cw), cw)
        src, dst = ((k_hbm, kbuf), (v_hbm, vbuf))[which]
        return pltpu.make_async_remote_copy(
            src_ref=src.at[:, cols],
            dst_ref=dst.at[blk, :, cols],
            send_sem=kv_send.at[k, c, which],
            recv_sem=kv_recv.at[k, c, which],
            device_id=blk_peers[k],
            device_id_type=MESH,
        )

    def start_chunk(c):
        for k in range(blks - 1):
            for which in range(2):
                kv_copy(k, c, which).start()

    for c in range(EARLY):
        start_chunk(c)
    if paired:

        @pl.when(blk == 1)
        def _():
            greet(barrier, wide)

    loads[0].wait()
    loads[1].wait()
    loads[3].wait()
    loads[4].wait()

    row = lax.broadcasted_iota(jnp.int32, (2 * HEADS, rows), 0)
    col = lax.broadcasted_iota(jnp.int32, (2 * HEADS, rows), 1)
    is_mid = row < HEADS
    mid_at = (row % per_dev) * MID_RATE

    def one_hot(h):
        mid_hit = is_mid & (row // per_dev == h // HALF) & (col == mid_at + mid_ref[h])
        far_hit = (row == HEADS + h) & (col == far_ref[h])
        return jnp.where(mid_hit | far_hit, 1.0, 0.0).astype(jnp.bfloat16)

    far_kv = jnp.zeros((HEADS, 2 * DH), jnp.float32)
    hots = []
    for g in range(HALF):
        lo = slice(g * DH, (g + 1) * DH)
        hi = slice((g + HALF) * DH, (g + HALF + 1) * DH)
        hot = jnp.concatenate([one_hot(g), one_hot(g + HALF)], axis=1)
        hots.append(hot)
        field = jnp.concatenate(
            [
                jnp.concatenate([kbuf[blk, :, lo], vbuf[blk, :, lo]], axis=1),
                jnp.concatenate([kbuf[blk, :, hi], vbuf[blk, :, hi]], axis=1),
            ],
            axis=0,
        )
        picked = dot_nn(hot, field)
        mid_kv = picked[:HEADS].astype(jnp.bfloat16)
        mid[place, blk, 0, :, lo] = mid_kv[:, :DH]
        mid[place, blk, 1, :, lo] = mid_kv[:, DH:]
        far_kv = far_kv + picked[HEADS:]
    far_kv = far_kv.astype(jnp.bfloat16)
    far[place, group, blk, 0] = far_kv[:, :DH]
    far[place, group, blk, 1] = far_kv[:, DH:]

    def remote(ref, send_sem, recv_sem, device):
        return pltpu.make_async_remote_copy(
            src_ref=ref,
            dst_ref=ref,
            send_sem=send_sem,
            recv_sem=recv_sem,
            device_id=device,
            device_id_type=MESH,
        )

    y_copies = []
    for k in range(blks - 1):
        for i, ref in enumerate((far.at[place, group, blk], mid.at[place, blk])):
            y_copies.append(remote(ref, y_send.at[k, i], y_recv.at[k, i], blk_peers[k]))
    for copy in y_copies:
        copy.start()
    for c in range(EARLY, n_chunks):
        start_chunk(c)

    if paired:

        @pl.when(blk == 1)
        def _():
            pl.semaphore_wait(barrier, len(wide))
            greet(wide_sem, blk_peers)

        @pl.when(blk == 0)
        def _():
            pl.semaphore_wait(wide_sem, 1)

    loads[2].wait()
    far_q = jnp.zeros((HEADS, DH), jnp.float32)
    for g in range(HALF):
        lo = slice(g * DH, (g + 1) * DH)
        hi = slice((g + HALF) * DH, (g + HALF + 1) * DH)
        field = jnp.concatenate([qbuf[:, lo], qbuf[:, hi]], axis=0)
        far_q = far_q + dot_nn(hots[g][HEADS:], field)
    far_q = far_q.astype(jnp.bfloat16)

    for copy in y_copies:
        copy.wait_recv()
    z_copies = [
        remote(far.at[place, group], z_send.at[k], z_recv.at[k], far_peers[k])
        for k in range(groups - 1)
    ]
    s_copies = [
        remote(mid.at[place], s_send.at[k], s_recv.at[k], span_peers[k]) for k in range(SPAN - 1)
    ]
    f_copies = [
        remote(far.at[place], f_send.at[k], f_recv.at[k], span_peers[k]) for k in range(SPAN - 1)
    ]
    for copy in z_copies + s_copies:
        copy.start()
    for copy in z_copies:
        copy.wait_recv()
    for copy in f_copies:
        copy.start()
    for copy in s_copies:
        copy.wait_recv()

    n_mid = SPAN * blks * 2 * per_dev
    mid_lane = lax.broadcasted_iota(jnp.int32, (rows, n_mid), 1) % (2 * per_dev) // per_dev
    mid_row = lax.broadcasted_iota(jnp.int32, (rows, n_mid), 0) % MID_RATE
    far_at = lax.broadcasted_iota(jnp.int32, (rows, DH), 0)

    def attend_far():
        n_far = segs * blks * HEADS
        far_keys = far[:, :, :, 0].reshape(n_far, DH)
        far_values = far[:, :, :, 1].reshape(n_far, DH)
        far_scores = dot_nt(far_q, far_keys)
        far_row = lax.broadcasted_iota(jnp.int32, (HEADS, n_far), 0)
        far_col = lax.broadcasted_iota(jnp.int32, (HEADS, n_far), 1)
        far_scores = jnp.where(far_col % HEADS == far_row, far_scores, very_low)
        far_top = jnp.max(far_scores, axis=1, keepdims=True)
        far_weights = jnp.exp2((far_scores - far_top) * SCALE)
        fden[...] = jnp.broadcast_to(jnp.sum(far_weights, axis=1, keepdims=True), (HEADS, DH))
        ftop[...] = jnp.broadcast_to(far_top, (HEADS, DH))
        fnum[...] = dot_nn(far_weights.astype(jnp.bfloat16), far_values)

    def attend(h, with_far):
        cols = pl.ds(pl.multiple_of(h * DH, DH), DH)
        mid_cols = pl.ds(pl.multiple_of(h % HALF * DH, DH), DH)
        query = qbuf[:, cols]
        dense_scores = dot_nt(query, kbuf[:, :, cols].reshape(blks * rows, DH))
        mid_scores = dot_nt(query, mid[:, :, 0, :, mid_cols].reshape(n_mid, DH))
        mid_ok = (mid_lane == h // HALF) & (mid_row == mid_ref[h])
        mid_scores = jnp.where(mid_ok, mid_scores, very_low)
        scores = jnp.concatenate([dense_scores, mid_scores], axis=1)
        top = jnp.max(scores, axis=1, keepdims=True)
        far_hit = far_at == far_ref[h]
        if with_far:
            far_low = jnp.where(far_hit, ftop[pl.ds(h, 1), :], very_low)
            wide_top = jnp.maximum(top, far_low)
            top = wide_top[:, :1]
        weights = jnp.exp2((scores - top) * SCALE)
        total = jnp.sum(weights, axis=1, keepdims=True)
        probs = weights.astype(jnp.bfloat16)
        yield
        mixed = dot_nn(probs[:, : blks * rows], vbuf[:, :, cols].reshape(blks * rows, DH))
        mixed = mixed + dot_nn(
            probs[:, blks * rows :], mid[:, :, 1, :, mid_cols].reshape(n_mid, DH)
        )
        if with_far:
            far_weight = jnp.exp2((far_low - wide_top) * SCALE)
            total = total + far_weight * fden[pl.ds(h, 1), :]
            mixed = mixed + far_weight * fnum[pl.ds(h, 1), :]
        else:
            for ref, value in ((rnum, mixed), (rtop, top), (rden, total)):
                kept = jnp.where(far_hit, value, 0.0)
                ref[pl.ds(h, 1), :] = jnp.sum(kept, axis=0, keepdims=True)
        out_ref[:, cols] = (mixed / total).astype(jnp.bfloat16)

    def merge_far():
        top = jnp.maximum(rtop[...], ftop[...])
        near_weight = jnp.exp2((rtop[...] - top) * SCALE)
        far_weight = jnp.exp2((ftop[...] - top) * SCALE)
        total = near_weight * rden[...] + far_weight * fden[...]
        rnum[...] = (near_weight * rnum[...] + far_weight * fnum[...]) / total

        def put(h, carry):
            cols = pl.ds(pl.multiple_of(h * DH, DH), DH)
            plain = out_ref[:, cols].astype(jnp.float32)
            merged = jnp.where(far_at == far_ref[h], rnum[pl.ds(h, 1), :], plain)
            out_ref[:, cols] = merged.astype(jnp.bfloat16)
            return carry

        lax.fori_loop(0, HEADS - LATE * CHUNK, put, 0, unroll=2)

    def await_chunk(c, which):
        for k in range(blks - 1):
            kv_copy(k, c, which).wait_recv()

    def run_chunk(c, with_far):
        await_chunk(c, 0)
        heads = [attend(c * CHUNK + j, with_far) for j in range(CHUNK)]
        for head in heads:
            next(head)
        await_chunk(c, 1)
        for head in heads:
            next(head, None)

    def chunk_step(c, carry):
        run_chunk(c, False)
        return carry

    for ref in (rnum, rtop, rden):
        ref[...] = jnp.ones_like(ref)
    lax.fori_loop(0, n_chunks - LATE, chunk_step, 0)
    for copy in f_copies:
        copy.wait_recv()
    attend_far()
    merge_far()
    for c in range(n_chunks - LATE, n_chunks):
        run_chunk(c, True)

    for copy in y_copies + s_copies + z_copies + f_copies:
        copy.wait_send()

    def finish(c, carry):
        for k in range(blks - 1):
            for which in range(2):
                kv_copy(k, c, which).wait_send()
        return carry

    lax.fori_loop(0, n_chunks, finish, 0)


def on_device(segs, blks, queries, keys, values, mid_offset, far_offset):
    rows, width = queries.shape
    groups = segs // SPAN
    n_chunks = HEADS // CHUNK
    bf16, f32 = jnp.bfloat16, jnp.float32
    dma = pltpu.SemaphoreType.DMA
    any_spec = pl.BlockSpec(memory_space=pl.ANY)
    return pl.pallas_call(
        functools.partial(kernel, segs, blks),
        out_shape=pltpu.VMEM((rows, width), bf16),
        in_specs=[any_spec] * 5,
        out_specs=pl.BlockSpec(memory_space=pltpu.VMEM),
        scratch_shapes=[
            pltpu.SMEM((HEADS,), jnp.int32),
            pltpu.SMEM((HEADS,), jnp.int32),
            pltpu.VMEM((rows, width), bf16),
            pltpu.VMEM((blks, rows, width), bf16),
            pltpu.VMEM((blks, rows, width), bf16),
            pltpu.VMEM((SPAN, blks, 2, HEADS, MIDW), bf16),
            pltpu.VMEM((SPAN, groups, blks, 2, HEADS, DH), bf16),
            pltpu.VMEM((HEADS, DH), f32),
            pltpu.VMEM((HEADS, DH), f32),
            pltpu.VMEM((HEADS, DH), f32),
            pltpu.VMEM((HEADS, DH), f32),
            pltpu.VMEM((HEADS, DH), f32),
            pltpu.VMEM((HEADS, DH), f32),
            pltpu.SemaphoreType.REGULAR,
            pltpu.SemaphoreType.REGULAR,
            dma((5,)),
            dma((blks - 1, n_chunks, 2)),
            dma((blks - 1, n_chunks, 2)),
            dma((blks - 1, 2)),
            dma((blks - 1, 2)),
            dma((SPAN - 1,)),
            dma((SPAN - 1,)),
            dma((groups - 1,)),
            dma((groups - 1,)),
            dma((SPAN - 1,)),
            dma((SPAN - 1,)),
        ],
        compiler_params=pltpu.CompilerParams(
            collective_id=0, has_side_effects=True, vmem_limit_bytes=62 * 1024 * 1024
        ),
    )(queries, keys, values, mid_offset, far_offset)


def solution(mesh):
    spec = P(("seg", "blk"), None)
    return jax.shard_map(
        functools.partial(on_device, mesh.shape["seg"], mesh.shape["blk"]),
        mesh=mesh,
        in_specs=(spec, spec, spec, P(), P()),
        out_specs=spec,
        check_vma=False,
    )
```
